1024 devices in a mesh: dp: 8 (over y, core), ctx: 16 (over z_hi, x), tp: 8 (over z_lo).
Axes of the slice: x: 4, y: 4, z: 32 (z_hi: 4, z_lo: 8; z = z_hi * 8 + z_lo), core: 2. Of those that a mesh axis runs over, the one named last changes fastest.
Arguments:
- queries: bfloat16 [128, 512, 4096], P(('dp', 'ctx'), None, 'tp'), may hold values from -400 to 400
- key_rows: bfloat16 [128, 512, 1024], P(('dp', 'ctx'), None, 'tp'), may hold values from -6 to 6
- value_rows: bfloat16 [128, 512, 1024], P(('dp', 'ctx'), None, 'tp'), may hold values from -6 to 6
- out_grad: bfloat16 [128, 512, 4096], P(('dp', 'ctx'), None, 'tp'), may hold values from -6 to 6
- inputs: bfloat16 [128, 512, 8192], P(('dp', 'ctx'), None, 'tp'), may hold values from -0.09375 to 0.09375
- doc_lengths: int32 [128, 16], P('dp'), may hold values from 1 to 40, 512 in all within a row
- doc_plan: int32 [128, 16], P('dp'), may hold values from 0 to 15, each once within a row
Outputs:
- query_grad: bfloat16 [128, 640, 4096], P(('dp', 'ctx'), None, 'tp')
- key_grad: bfloat16 [128, 640, 1024], P(('dp', 'ctx'), None, 'tp')
- value_grad: bfloat16 [128, 640, 1024], P(('dp', 'ctx'), None, 'tp')
- weight_grad: float32 [8192, 1024], P(('tp', 'dp', 'ctx'))
The draws below stay inside these ranges and needn't reach their ends.
Inputs may be any that keep to these rules, and one draw needn't show every extreme that they name: `doc_lengths`: each row sums to 512; every document has at most 40 tokens, and one of each row has exactly 40. Each row is a permutation: document d of sequence s goes to context index doc_plan[s, d] of the same data group.
All inputs are finite; a program needn't handle non-finite values.
Results may differ from the reference program's by a relative error of at most 0.012.
Values may be sent and summed in bfloat16 or wider, within the bound.
No kernel may reach another device: no remote copies, remote signals or barrier semaphores. Data moves between devices by JAX's collectives and lax.ppermute only.
A program may use at most 32 MiB of HBM per device.

```python
import math
import jax
import jax.numpy as jnp
import numpy as np
from jax import lax

D = 8192
HEADS = 32
KVH = 8
HD = 128
L = 512
NDOC = 16
CAP = 40
RECV = 640
SEQS = 128


def pair_draw(key):
    group_size = HEADS // KVH
    base_key = jax.random.fold_in(key, 71)
    key_first, key_second = jax.random.split(base_key, 2)
    keys_raw = jnp.clip(jax.random.normal(key_first, (SEQS, L, KVH, HD), jnp.float32), -6.0, 6.0)
    query_raw = jnp.clip(jax.random.normal(key_second, (SEQS, L, KVH, group_size, HD), jnp.float32), -6.0, 6.0)
    keys_out = keys_raw
    query_out = query_raw
    return (query_out.reshape(SEQS, L, HEADS * HD), keys_out.reshape(SEQS, L, KVH * HD))


def draw_queries(key, part):
    return pair_draw(key)[0].astype(jnp.bfloat16)


def draw_key_rows(key, part):
    return pair_draw(key)[1].astype(jnp.bfloat16)


def with_spikes(array, own_key, source, target, blocks, factor):
    owner, partner = [(jnp.arange(array.shape[axis_at]) // (array.shape[axis_at] // blocks)).reshape([-1 if axis == axis_at else 1 for axis in range(array.ndim)]) for axis_at in (source, target)]
    chosen = jax.random.permutation(own_key, blocks)[partner]
    strong = (owner == chosen) | (owner == (partner + blocks // 2) % blocks)
    return jnp.where(strong, factor * array, array)


def steps_of(stream_key, dims, pieces, low, high):
    loudness = 1.0
    for dim, shards_of in pieces:
        heights = jax.random.uniform(jax.random.fold_in(jax.random.fold_in(stream_key, 6), dim), (shards_of,), jnp.float32, low / len(pieces), high / len(pieces))
        loudness = loudness * jnp.repeat(jnp.exp(heights), dims[dim] // shards_of).reshape((-1,) + (1,) * (len(dims) - 1 - dim))
    return loudness


def split_up(amount, total, reach, lean):
    weights = [(1 << 20) // math.isqrt(grade ** lean) + 1 for grade in range(2, amount + 1)]
    rest, counts = total - reach - (amount - 1), [1] * (amount - 1)
    while rest > 0:
        movable = [i for i in range(amount - 1) if counts[i] < reach]
        mass, budget = sum([weights[i] for i in movable]), rest
        for i in movable:
            addition = min(reach - counts[i], max(1, budget * weights[i] // mass), rest)
            counts[i] = counts[i] + addition
            rest = rest - addition
    return np.array([reach] + counts)


def ragged(key, number_of, total, reach, skew):
    if number_of == 2:
        one = jax.random.randint(key, (), max(1, total - reach), min(reach, total - 1) + 1)
        return jnp.stack([one, total - one])
    tallies = jnp.asarray(split_up(number_of, total, reach, skew), jnp.int32)
    pairs = (number_of - 1) // 2
    donor, receiver = tallies[1:1 + 2 * pairs:2], tallies[2:2 + 2 * pairs:2]
    slack = jnp.minimum(donor - 1, reach - receiver)
    moved = jax.random.randint(jax.random.fold_in(key, 1), (pairs,), 0, 1 << 20) % (slack + 1)
    tallies = tallies.at[1:1 + 2 * pairs:2].set(donor - moved).at[2:2 + 2 * pairs:2].set(receiver + moved)
    return tallies[jax.random.permutation(jax.random.fold_in(key, 2), number_of)]


def gaussian(own_key, extent, width, reach, cuts=(), held_as=jnp.bfloat16):
    gain = steps_of(own_key, extent, cuts, -0.22, 0.18) if cuts else 1.0
    entries = jax.random.normal(own_key, extent, jnp.float32) * width * gain
    return jnp.minimum(jnp.maximum(entries, -reach), reach).astype(held_as)


def bell_draw_with(rng, dims, deviation, limit, shards, heavy, kind=jnp.bfloat16):
    entries = deviation * jax.random.normal(rng, dims, jnp.float32)
    if shards:
        entries = entries * steps_of(rng, dims, shards, -0.22, 0.18)
    return jnp.clip(with_spikes(entries, jax.random.fold_in(rng, 3), *heavy), -limit, limit).astype(kind)


def setup_inputs(seed: int = 0) -> dict:
    key_of = jax.random.split(jax.random.key(seed), 8)
    return {
        "queries": draw_queries(jax.random.fold_in(key_of[7], 71), 0),
        "key_rows": draw_key_rows(jax.random.fold_in(key_of[7], 71), 0),
        "value_rows": gaussian(key_of[2], (SEQS, L, KVH * HD), 1.0, 6.0, ((0, 128), (2, 8))),
        "out_grad": gaussian(key_of[3], (SEQS, L, HEADS * HD), 1.0, 6.0, ((0, 128), (2, 8))),
        "inputs": bell_draw_with(key_of[4], (SEQS, L, D), (1.0 / (SEQS * L) ** 0.5), 0.09375, ((0, 128), (2, 8)), (0, 2, 128, 5.5)),
        "doc_lengths": jax.vmap(lambda own: ragged(own, NDOC, L, CAP, 2))(jax.random.split(key_of[5], SEQS)).reshape((SEQS, NDOC)).astype(jnp.int32),
        "doc_plan": jax.vmap(lambda own: jax.random.permutation(own, NDOC))(jax.random.split(key_of[6], SEQS)).reshape((SEQS, NDOC)).astype(jnp.int32),
    }


def block_grads(query_rows, key_part, value_part, grad_rows, allowed):
    score_scale = HD ** -0.5
    highest = lax.Precision.HIGHEST
    scores = jnp.einsum('nrcgh,nsch->ncgrs', query_rows, key_part, precision=highest) * score_scale
    scores = jnp.where(allowed[:, None, None, :, :] == 1, scores, -jnp.inf)
    largest = jnp.max(scores, axis=4, keepdims=True)
    raised = jnp.exp(scores - largest)
    weights = raised / jnp.sum(raised, axis=4, keepdims=True)
    weights_low = lax.optimization_barrier(weights.astype(jnp.bfloat16)).astype(jnp.float32)
    attended = jnp.einsum('ncgrs,nsch->nrcgh', weights_low, value_part, precision=highest)
    row_delta = jnp.einsum('nrcgh,nrcgh->ncgr', grad_rows, attended, precision=highest)
    prob_grad = jnp.einsum('nrcgh,nsch->ncgrs', grad_rows, value_part, precision=highest)
    dscore = (weights * (prob_grad - row_delta[..., None])).astype(jnp.bfloat16)
    dscore = lax.optimization_barrier(dscore).astype(jnp.float32)
    query_grad = jnp.einsum('ncgrs,nsch->nrcgh', dscore, key_part, precision=highest) * score_scale
    key_grad = jnp.einsum('ncgrs,nrcgh->nsch', dscore, query_rows, precision=highest) * score_scale
    value_grad = jnp.einsum('ncgrs,nrcgh->nsch', weights_low, grad_rows, precision=highest)
    return query_grad, key_grad, value_grad


def reference(queries, key_rows, value_rows, out_grad, inputs, doc_lengths, doc_plan):
    group_size = HEADS // KVH
    starts = jnp.cumsum(doc_lengths, axis=1) - doc_lengths
    doc_ids = jnp.arange(NDOC, dtype=jnp.int32)
    matches = (doc_plan[:, None, :] == doc_ids[None, :, None]).astype(jnp.int32)
    inverse = jnp.sum(doc_ids[None, None, :] * matches, axis=2).astype(jnp.int32)
    offsets = jnp.arange(CAP, dtype=jnp.int32)
    causal = offsets[None, :] <= offsets[:, None]
    diagonal = offsets[None, :] == offsets[:, None]

    def one_target(running, target_seq):
        group_base = (target_seq // NDOC) * NDOC
        target = target_seq % NDOC
        sources = (group_base + doc_ids).astype(jnp.int32)
        chosen = inverse[sources, target]
        length = doc_lengths[sources, chosen]
        first_tok = starts[sources, chosen]
        filled = offsets[None, :] < length[:, None]
        position = jnp.minimum(first_tok[:, None] + offsets[None, :], L - 1).astype(jnp.int32)

        def gather_rows(source):
            picked = source[sources[:, None], position]
            return jnp.where(filled[:, :, None], picked, jnp.zeros((), source.dtype))

        query_recv = gather_rows(queries).astype(jnp.float32).reshape(NDOC, CAP, KVH, group_size, HD)
        key_recv = gather_rows(key_rows).astype(jnp.float32).reshape(NDOC, CAP, KVH, HD)
        value_recv = gather_rows(value_rows).astype(jnp.float32).reshape(NDOC, CAP, KVH, HD)
        grad_recv = gather_rows(out_grad).astype(jnp.float32).reshape(NDOC, CAP, KVH, group_size, HD)
        allowed = (causal[None] & (filled[:, :, None] | diagonal[None])).astype(jnp.int32)
        query_grad, key_grad, value_grad = block_grads(query_recv, key_recv, value_recv, grad_recv, allowed)
        query_out = query_grad.reshape(RECV, HEADS * HD).astype(jnp.bfloat16)
        key_out = key_grad.reshape(RECV, KVH * HD).astype(jnp.bfloat16)
        value_out = value_grad.reshape(RECV, KVH * HD).astype(jnp.bfloat16)
        input_recv = gather_rows(inputs).reshape(RECV, D).astype(jnp.float32)
        running = running + jnp.dot(input_recv.T, value_out.astype(jnp.float32), precision=lax.Precision.HIGHEST)
        return running, (query_out, key_out, value_out)

    summed, outputs = lax.scan(one_target, jnp.zeros((D, KVH * HD), jnp.float32), jnp.arange(SEQS, dtype=jnp.int32))
    return outputs[0], outputs[1], outputs[2], summed
```

```python
import functools

import jax
import jax.numpy as jnp
from jax import lax
from jax.experimental import pallas as pl
from jax.experimental.pallas import tpu as pltpu
from jax.sharding import Mesh, PartitionSpec as P


HD = 128
GROUP = 4
DOCS = 4
NEG = -1e30
LOW = jnp.bfloat16


def dot(a, b):
    return jnp.dot(a, b, preferred_element_type=jnp.float32)


def nt_dot(a, b):
    return lax.dot_general(a, b, (((1,), (1,)), ((), ())), preferred_element_type=jnp.float32)


def tn_dot(a, b):
    return lax.dot_general(a, b, (((0,), (0,)), ((), ())), preferred_element_type=jnp.float32)


def block_of(ids, capacity):
    block = jnp.zeros_like(ids)
    for d in range(1, DOCS):
        block = block + (ids >= d * capacity).astype(jnp.int32)
    return block


def iotas(rows, cols):
    return (
        lax.broadcasted_iota(jnp.int32, (rows, cols), 0),
        lax.broadcasted_iota(jnp.int32, (rows, cols), 1),
    )


def causal_mask(capacity):
    tile = DOCS * capacity
    rows, cols = iotas(tile, tile)
    return (cols <= rows) & (block_of(rows, capacity) == block_of(cols, capacity))


def one_hot(condition):
    return jnp.where(condition, 1.0, 0.0).astype(LOW)


def lane_maps(capacity):
    tile = DOCS * capacity
    cols, lanes = iotas(tile, HD)
    within = cols - capacity * block_of(cols, capacity)
    half = HD // 2
    upright = [one_hot(lanes == within), one_hot(lanes == within + half)]
    turned = [one_hot(lanes == capacity - within), one_hot(lanes == capacity - within + half)]
    return upright, turned


def flip_map(capacity):
    tile = DOCS * capacity
    rows, cols = iotas(tile, tile)
    block = block_of(rows, capacity)
    within = rows - capacity * block
    return one_hot(cols == block * capacity + (capacity - 1) - within)


def attend_kernel(
    index_ref,
    lengths_ref,
    plan_ref,
    query_hbm,
    key_hbm,
    value_hbm,
    grad_hbm,
    packed_ref,
    tokens_ref,
    query_ref,
    key_ref,
    value_ref,
    grad_ref,
    place_ref,
    sums_ref,
    sems,
):
    copies = [
        pltpu.make_async_copy(source, target, sems.at[i])
        for i, (source, target) in enumerate(
            (
                (query_hbm, query_ref),
                (key_hbm, key_ref),
                (value_hbm, value_ref),
                (grad_hbm, grad_ref),
            )
        )
    ]
    for copy in copies:
        copy.start()
    seq_len = query_ref.shape[0]
    docs = lengths_ref.shape[1]
    capacity = packed_ref.shape[0] // docs
    tile = DOCS * capacity
    own = index_ref[0]
    scale = HD ** (-0.5)

    offsets = lax.broadcasted_iota(jnp.int32, (capacity, HD), 0)
    start = jnp.int32(0)
    for d in range(docs):
        length = lengths_ref[own, d]
        target = plan_ref[own, d]
        place_ref[pl.ds(pl.multiple_of(target * capacity, 8), capacity), :] = jnp.where(
            offsets < length, start + offsets, -1
        )
        start = start + length

    bias = jnp.where(causal_mask(capacity), 0.0, NEG)
    bias = jnp.concatenate([bias] * GROUP, axis=0)
    upright, turned = lane_maps(capacity)
    flip = flip_map(capacity)
    for copy in copies:
        copy.wait()
    for part in range(docs // DOCS):
        here = slice(part * tile, (part + 1) * tile)
        place = jnp.concatenate([place_ref[here, :]] * (seq_len // HD), axis=1)
        pick = one_hot(place == lax.broadcasted_iota(jnp.int32, (tile, seq_len), 1))
        query = dot(pick, query_ref[...]).astype(LOW)
        grad = dot(pick, grad_ref[...]).astype(LOW)
        key = dot(pick, key_ref[...]).astype(LOW)
        value = dot(pick, value_ref[...]).astype(LOW)
        query = jnp.concatenate([query[:, h * HD : (h + 1) * HD] for h in range(GROUP)], axis=0)
        grad = jnp.concatenate([grad[:, h * HD : (h + 1) * HD] for h in range(GROUP)], axis=0)
        scores = nt_dot(query, key) * scale + bias
        raised = jnp.exp(scores - jnp.max(scores, axis=1, keepdims=True))
        probs = raised / jnp.sum(raised, axis=1, keepdims=True)
        probs_low = probs.astype(LOW)
        prob_grad = nt_dot(grad, value)
        row_delta = jnp.sum(probs_low.astype(jnp.float32) * prob_grad, axis=1, keepdims=True)
        dscore = (probs * (prob_grad - row_delta)).astype(LOW)
        value_grad = tn_dot(probs_low, grad).astype(LOW)
        sums = tn_dot(pick, value_grad)
        if part == 0:
            sums_ref[...] = sums
        else:
            sums_ref[...] += sums
        heads = [dscore[h * tile : (h + 1) * tile, :] for h in range(GROUP)]
        below = dot(heads[0], upright[0]) + dot(heads[1], upright[1])
        above = (dot(heads[2], turned[0]) + dot(heads[3], turned[1])).astype(LOW)
        packed_ref[here, 0:HD] = key
        packed_ref[here, HD : 2 * HD] = (tn_dot(dscore, query) * scale).astype(LOW)
        packed_ref[here, 2 * HD : 3 * HD] = value_grad
        packed_ref[here, 3 * HD : 4 * HD] = (below + dot(flip, above)).astype(LOW)
    tokens_ref[...] = sums_ref[...].astype(LOW)


def attend(index, lengths, plan, query, key, value, grad):
    seq_len, width = query.shape
    docs = lengths.shape[1]
    packed = docs * (5 * seq_len // (4 * docs))
    smem = pl.BlockSpec(memory_space=pltpu.SMEM)
    vmem = pl.BlockSpec(memory_space=pltpu.VMEM)
    hbm = pl.BlockSpec(memory_space=pl.ANY)
    return pl.pallas_call(
        attend_kernel,
        out_shape=(
            jax.ShapeDtypeStruct((packed, 4 * HD), LOW),
            jax.ShapeDtypeStruct((seq_len, HD), LOW),
        ),
        in_specs=[smem, smem, smem, hbm, hbm, hbm, hbm],
        out_specs=(vmem, vmem),
        scratch_shapes=[
            pltpu.VMEM((seq_len, width), LOW),
            pltpu.VMEM((seq_len, HD), LOW),
            pltpu.VMEM((seq_len, HD), LOW),
            pltpu.VMEM((seq_len, width), LOW),
            pltpu.VMEM((packed, HD), jnp.int32),
            pltpu.VMEM((seq_len, HD), jnp.float32),
            pltpu.SemaphoreType.DMA((4,)),
        ],
        compiler_params=pltpu.CompilerParams(vmem_limit_bytes=60 << 20),
        name="attend",
    )(index, lengths, plan, query, key, value, grad)


def finish_kernel(capacity, packed_ref, query_out, key_out, value_out):
    scale = HD ** (-0.5)
    mask = causal_mask(capacity)
    upright, turned = lane_maps(capacity)
    key = packed_ref[:, 0:HD]
    below = packed_ref[:, 3 * HD : 4 * HD]
    above = dot(flip_map(capacity), below).astype(LOW)
    for h, (half, lanes) in enumerate(
        ((below, upright[0]), (below, upright[1]), (above, turned[0]), (above, turned[1]))
    ):
        dscore = jnp.where(mask, nt_dot(half, lanes), 0.0).astype(LOW)
        query_out[:, h * HD : (h + 1) * HD] = (dot(dscore, key) * scale).astype(LOW)
    key_out[...] = packed_ref[:, HD : 2 * HD]
    value_out[...] = packed_ref[:, 2 * HD : 3 * HD]


def finish(received, capacity):
    rows = received.shape[0]
    tile = DOCS * capacity

    def spec(width):
        return pl.BlockSpec((tile, width), lambda i: (i, 0))

    return pl.pallas_call(
        functools.partial(finish_kernel, capacity),
        grid=(rows // tile,),
        out_shape=(
            jax.ShapeDtypeStruct((rows, GROUP * HD), LOW),
            jax.ShapeDtypeStruct((rows, HD), LOW),
            jax.ShapeDtypeStruct((rows, HD), LOW),
        ),
        in_specs=[spec(4 * HD)],
        out_specs=(spec(GROUP * HD), spec(HD), spec(HD)),
        compiler_params=pltpu.CompilerParams(vmem_limit_bytes=16 << 20),
        name="finish",
    )(received)


def shift(value, axis, step):
    n = lax.axis_size(axis)
    return lax.ppermute(value, axis, [(i, (i + step) % n) for i in range(n)])


def fold(total, axis, dim):
    n = lax.axis_size(axis)
    me = lax.axis_index(axis)
    summed = lax.dynamic_index_in_dim(total, me, dim, keepdims=False)
    for step in range(1, n):
        piece = lax.dynamic_index_in_dim(total, lax.rem(me + step, n), dim, keepdims=False)
        summed = summed + shift(piece.astype(LOW), axis, step).astype(jnp.float32)
    return summed


def fold_far(total, axis):
    me = lax.axis_index(axis)
    first, second = jnp.bitwise_xor(me, 1), 3 - me

    def at(value, i):
        return lax.dynamic_index_in_dim(value, i, 0, keepdims=False)

    away = jnp.stack([at(total, first), at(total, 3 - first)])
    came = lax.ppermute(away.astype(LOW), axis, [(i, i ^ 1) for i in range(4)])
    mine = at(total, me) + came[0].astype(jnp.float32)
    other = at(total, second) + came[1].astype(jnp.float32)
    back = lax.ppermute(other.astype(LOW), axis, [(i, 3 - i) for i in range(4)])
    return mine + back.astype(jnp.float32)


def shards(queries, key_rows, value_rows, out_grad, inputs, doc_lengths, doc_plan):
    own = lax.axis_index(("zhi", "x")).astype(jnp.int32).reshape(1)
    packed, tokens = attend(
        own, doc_lengths, doc_plan, queries[0], key_rows[0], value_rows[0], out_grad[0]
    )
    near = lax.axis_size("zr")
    across = shift(tokens, "zq", 1)
    blocks = [tokens] + [shift(tokens, "zr", k) for k in range(1, near)]
    blocks += [across]
    for k in range(1, near):
        blocks += [shift(across, "zr", k)]
    received = lax.all_to_all(packed, ("zhi", "x"), split_axis=0, concat_axis=0, tiled=True)
    values = jnp.concatenate(blocks, axis=1)
    rows, features = inputs.shape[1:]
    width = values.shape[1]
    ny, nc, nz, nx = (lax.axis_size(a) for a in ("y", "core", "zhi", "x"))
    halves = inputs.reshape(rows, ny, nc, features // (ny * nc))
    core = lax.axis_index("core")

    def term(i):
        part = lax.dynamic_index_in_dim(halves, i, 2, keepdims=False).reshape(rows, features // nc)
        return tn_dot(part, values)

    came = shift(term(1 - core).astype(LOW), "core", 1)
    kept = lax.optimization_barrier(term(core))
    total = kept + came.astype(jnp.float32)
    total = total.reshape(ny, nz, nx, features // (ny * nc * nz * nx), width)
    total = fold(total, "x", 2)
    total = fold(total, "y", 0)
    total = fold_far(total, "zhi")
    total = total.reshape(-1, 2 * near, HD)
    zq, zr = lax.axis_index("zq"), lax.axis_index("zr")
    block = jnp.arange(2 * near)
    source = jnp.bitwise_and(zr - block, near - 1) + near * (block // near != zq)
    total = jnp.take(total, source, axis=1).reshape(-1, width)
    query_grad, key_grad, value_grad = finish(received, packed.shape[0] // doc_plan.shape[1])
    return (query_grad[None], key_grad[None], value_grad[None], total)


def solution(mesh):
    fine = Mesh(mesh.devices.reshape(4, 2, 4, 4, 2, 4), ("y", "core", "zhi", "x", "zq", "zr"))
    tokens = P(("y", "core", "zhi", "x"), None, ("zq", "zr"))
    groups = P(("y", "core"), None)

    return jax.shard_map(
        shards,
        mesh=fine,
        in_specs=(tokens, tokens, tokens, tokens, tokens, groups, groups),
        out_specs=(tokens, tokens, tokens, P(("zq", "zr", "y", "core", "zhi", "x"), None)),
        check_vma=False,
    )
```

```python
import functools

import jax
import jax.numpy as jnp
from jax import lax
from jax.experimental import pallas as pl
from jax.experimental.pallas import tpu as pltpu
from jax.sharding import Mesh, PartitionSpec as P


HD = 128
GROUP = 4
DOCS = 4
NEG = -1e30
LOW = jnp.bfloat16


def dot(a, b):
    return jnp.dot(a, b, preferred_element_type=jnp.float32)


def nt_dot(a, b):
    return lax.dot_general(a, b, (((1,), (1,)), ((), ())), preferred_element_type=jnp.float32)


def tn_dot(a, b):
    return lax.dot_general(a, b, (((0,), (0,)), ((), ())), preferred_element_type=jnp.float32)


def block_of(ids, capacity):
    block = jnp.zeros_like(ids)
    for d in range(1, DOCS):
        block = block + (ids >= d * capacity).astype(jnp.int32)
    return block


def iotas(rows, cols):
    return (
        lax.broadcasted_iota(jnp.int32, (rows, cols), 0),
        lax.broadcasted_iota(jnp.int32, (rows, cols), 1),
    )


def causal_mask(capacity):
    tile = DOCS * capacity
    rows, cols = iotas(tile, tile)
    return (cols <= rows) & (block_of(rows, capacity) == block_of(cols, capacity))


def one_hot(condition):
    return jnp.where(condition, 1.0, 0.0).astype(LOW)


def lane_maps(capacity):
    tile = DOCS * capacity
    cols, lanes = iotas(tile, HD)
    within = cols - capacity * block_of(cols, capacity)
    half = HD // 2
    upright = [one_hot(lanes == within), one_hot(lanes == within + half)]
    turned = [one_hot(lanes == capacity - within), one_hot(lanes == capacity - within + half)]
    return upright, turned


def flip_map(capacity):
    tile = DOCS * capacity
    rows, cols = iotas(tile, tile)
    block = block_of(rows, capacity)
    within = rows - capacity * block
    return one_hot(cols == block * capacity + (capacity - 1) - within)


def place_rows(index_ref, lengths_ref, plan_ref, place_ref, capacity):
    own = index_ref[0]
    offsets = lax.broadcasted_iota(jnp.int32, (capacity, HD), 0)
    start = jnp.int32(0)
    for d in range(lengths_ref.shape[1]):
        length = lengths_ref[own, d]
        target = plan_ref[own, d]
        place_ref[pl.ds(pl.multiple_of(target * capacity, 8), capacity), :] = jnp.where(
            offsets < length, start + offsets, -1
        )
        start = start + length


def fetch(pairs, sems):
    copies = [
        pltpu.make_async_copy(source, target, sems.at[i])
        for i, (source, target) in enumerate(pairs)
    ]
    for copy in copies:
        copy.start()
    return copies


def picker(place_ref, here, seq_len):
    place = jnp.concatenate([place_ref[here, :]] * (seq_len // HD), axis=1)
    return one_hot(place == lax.broadcasted_iota(jnp.int32, place.shape, 1))


def by_head(rows):
    return jnp.concatenate([rows[:, h * HD : (h + 1) * HD] for h in range(GROUP)], axis=0)


def softmax_bias(capacity):
    return jnp.concatenate([jnp.where(causal_mask(capacity), 0.0, NEG)] * GROUP, axis=0)


def softmax(query, key, bias):
    scores = nt_dot(query, key) * HD ** (-0.5) + bias
    raised = jnp.exp(scores - jnp.max(scores, axis=1, keepdims=True))
    return raised / jnp.sum(raised, axis=1, keepdims=True)


def tokens_kernel(
    index_ref,
    lengths_ref,
    plan_ref,
    query_hbm,
    key_hbm,
    grad_hbm,
    tokens_ref,
    query_ref,
    key_ref,
    grad_ref,
    place_ref,
    sems,
):
    copies = fetch(((query_hbm, query_ref), (key_hbm, key_ref), (grad_hbm, grad_ref)), sems)
    seq_len = query_ref.shape[0]
    capacity = place_ref.shape[0] // lengths_ref.shape[1]
    tile = DOCS * capacity
    place_rows(index_ref, lengths_ref, plan_ref, place_ref, capacity)
    bias = softmax_bias(capacity)
    for copy in copies:
        copy.wait()
    sums = jnp.zeros(tokens_ref.shape, jnp.float32)
    for part in range(place_ref.shape[0] // tile):
        pick = picker(place_ref, slice(part * tile, (part + 1) * tile), seq_len)
        query = by_head(dot(pick, query_ref[...]).astype(LOW))
        grad = by_head(dot(pick, grad_ref[...]).astype(LOW))
        key = dot(pick, key_ref[...]).astype(LOW)
        probs_low = softmax(query, key, bias).astype(LOW)
        sums += tn_dot(pick, tn_dot(probs_low, grad).astype(LOW))
    tokens_ref[...] = sums.astype(LOW)


def attend_kernel(
    index_ref,
    lengths_ref,
    plan_ref,
    query_hbm,
    key_hbm,
    value_hbm,
    grad_hbm,
    packed_ref,
    query_ref,
    key_ref,
    value_ref,
    grad_ref,
    place_ref,
    sems,
):
    copies = fetch(
        (
            (query_hbm, query_ref),
            (key_hbm, key_ref),
            (value_hbm, value_ref),
            (grad_hbm, grad_ref),
        ),
        sems,
    )
    seq_len = query_ref.shape[0]
    capacity = place_ref.shape[0] // lengths_ref.shape[1]
    tile = DOCS * capacity
    scale = HD ** (-0.5)
    place_rows(index_ref, lengths_ref, plan_ref, place_ref, capacity)
    bias = softmax_bias(capacity)
    upright, turned = lane_maps(capacity)
    flip = flip_map(capacity)
    for copy in copies:
        copy.wait()
    for part in range(place_ref.shape[0] // tile):
        here = slice(part * tile, (part + 1) * tile)
        pick = picker(place_ref, here, seq_len)
        query = by_head(dot(pick, query_ref[...]).astype(LOW))
        grad = by_head(dot(pick, grad_ref[...]).astype(LOW))
        key = dot(pick, key_ref[...]).astype(LOW)
        value = dot(pick, value_ref[...]).astype(LOW)
        probs = softmax(query, key, bias)
        probs_low = probs.astype(LOW)
        prob_grad = nt_dot(grad, value)
        row_delta = jnp.sum(probs_low.astype(jnp.float32) * prob_grad, axis=1, keepdims=True)
        dscore = (probs * (prob_grad - row_delta)).astype(LOW)
        heads = [dscore[h * tile : (h + 1) * tile, :] for h in range(GROUP)]
        below = dot(heads[0], upright[0]) + dot(heads[1], upright[1])
        above = (dot(heads[2], turned[0]) + dot(heads[3], turned[1])).astype(LOW)
        packed_ref[here, 0:HD] = key
        packed_ref[here, HD : 2 * HD] = (tn_dot(dscore, query) * scale).astype(LOW)
        packed_ref[here, 2 * HD : 3 * HD] = tn_dot(probs_low, grad).astype(LOW)
        packed_ref[here, 3 * HD : 4 * HD] = (below + dot(flip, above)).astype(LOW)


def local_call(kernel, plan_of, arrays, out_shape, flops):
    seq_len = arrays[0].shape[0]
    docs = plan_of[1].shape[1]
    packed = docs * (5 * seq_len // (4 * docs))
    smem = pl.BlockSpec(memory_space=pltpu.SMEM)
    moved = sum(2 * a.size for a in arrays)
    return pl.pallas_call(
        kernel,
        out_shape=out_shape(packed),
        in_specs=[smem] * 3 + [pl.BlockSpec(memory_space=pl.ANY)] * len(arrays),
        out_specs=pl.BlockSpec(memory_space=pltpu.VMEM),
        scratch_shapes=[pltpu.VMEM(a.shape, LOW) for a in arrays]
        + [pltpu.VMEM((packed, HD), jnp.int32), pltpu.SemaphoreType.DMA((len(arrays),))],
        compiler_params=pltpu.CompilerParams(vmem_limit_bytes=60 << 20),
        cost_estimate=pl.CostEstimate(flops=flops, bytes_accessed=moved, transcendentals=400000),
    )(*plan_of, *arrays)


def value_tokens(plan_of, query, key, grad):
    return local_call(
        tokens_kernel,
        plan_of,
        (query, key, grad),
        lambda packed: jax.ShapeDtypeStruct(key.shape, LOW),
        10**9,
    )


def attend(plan_of, query, key, value, grad):
    return local_call(
        attend_kernel,
        plan_of,
        (query, key, value, grad),
        lambda packed: jax.ShapeDtypeStruct((packed, 4 * HD), LOW),
        2 * 10**9,
    )


def finish_kernel(capacity, packed_ref, query_out, key_out, value_out):
    scale = HD ** (-0.5)
    mask = causal_mask(capacity)
    upright, turned = lane_maps(capacity)
    key = packed_ref[:, 0:HD]
    below = packed_ref[:, 3 * HD : 4 * HD]
    above = dot(flip_map(capacity), below).astype(LOW)
    for h, (half, lanes) in enumerate(
        ((below, upright[0]), (below, upright[1]), (above, turned[0]), (above, turned[1]))
    ):
        dscore = jnp.where(mask, nt_dot(half, lanes), 0.0).astype(LOW)
        query_out[:, h * HD : (h + 1) * HD] = (dot(dscore, key) * scale).astype(LOW)
    key_out[...] = packed_ref[:, HD : 2 * HD]
    value_out[...] = packed_ref[:, 2 * HD : 3 * HD]


def finish(received, capacity):
    rows = received.shape[0]
    tile = DOCS * capacity

    def spec(width):
        return pl.BlockSpec((tile, width), lambda i: (i, 0))

    return pl.pallas_call(
        functools.partial(finish_kernel, capacity),
        grid=(rows // tile,),
        out_shape=(
            jax.ShapeDtypeStruct((rows, GROUP * HD), LOW),
            jax.ShapeDtypeStruct((rows, HD), LOW),
            jax.ShapeDtypeStruct((rows, HD), LOW),
        ),
        in_specs=[spec(4 * HD)],
        out_specs=(spec(GROUP * HD), spec(HD), spec(HD)),
        compiler_params=pltpu.CompilerParams(vmem_limit_bytes=16 << 20),
        name="finish",
    )(received)


def term_kernel(core_ref, inputs_ref, *refs):
    *block_refs, away_ref, kept_ref = refs
    values = jnp.concatenate([ref[...] for ref in block_refs], axis=1)
    cores = inputs_ref.shape[1] // away_ref.shape[0]
    for out_ref, which in ((away_ref, cores - 1 - core_ref[0]), (kept_ref, core_ref[0])):
        for y in range(out_ref.shape[0] // HD):
            part = inputs_ref[:, pl.ds(pl.multiple_of((y * cores + which) * HD, HD), HD)]
            out_ref[y * HD : (y + 1) * HD, :] = tn_dot(part, values).astype(out_ref.dtype)


def terms(core, inputs, blocks, cores):
    rows, width = inputs.shape[1] // cores, sum(b.shape[1] for b in blocks)
    return pl.pallas_call(
        term_kernel,
        out_shape=(
            jax.ShapeDtypeStruct((rows, width), LOW),
            jax.ShapeDtypeStruct((rows, width), jnp.float32),
        ),
        in_specs=[pl.BlockSpec(memory_space=pltpu.SMEM)]
        + [pl.BlockSpec(memory_space=pltpu.VMEM)] * (1 + len(blocks)),
        out_specs=(pl.BlockSpec(memory_space=pltpu.VMEM),) * 2,
        compiler_params=pltpu.CompilerParams(vmem_limit_bytes=24 << 20),
        name="terms",
    )(core, inputs, *blocks)


def shift(value, axis, step):
    n = lax.axis_size(axis)
    return lax.ppermute(value, axis, [(i, (i + step) % n) for i in range(n)])


def fold(total, axis, dim):
    n = lax.axis_size(axis)
    me = lax.axis_index(axis)
    summed = lax.dynamic_index_in_dim(total, me, dim, keepdims=False)
    for step in range(1, n):
        piece = lax.dynamic_index_in_dim(total, lax.rem(me + step, n), dim, keepdims=False)
        summed = summed + shift(piece.astype(LOW), axis, step).astype(jnp.float32)
    return summed


def fold_far(total, axis):
    me = lax.axis_index(axis)
    first, second = jnp.bitwise_xor(me, 1), 3 - me

    def at(value, i):
        return lax.dynamic_index_in_dim(value, i, 0, keepdims=False)

    away = jnp.stack([at(total, first), at(total, 3 - first)])
    came = lax.ppermute(away.astype(LOW), axis, [(i, i ^ 1) for i in range(4)])
    mine = at(total, me) + came[0].astype(jnp.float32)
    other = at(total, second) + came[1].astype(jnp.float32)
    back = lax.ppermute(other.astype(LOW), axis, [(i, 3 - i) for i in range(4)])
    return mine + back.astype(jnp.float32)


def shards(queries, key_rows, value_rows, out_grad, inputs, doc_lengths, doc_plan):
    own = lax.axis_index(("zhi", "x")).astype(jnp.int32).reshape(1)
    plan_of = (own, doc_lengths, doc_plan)
    tokens = value_tokens(plan_of, queries[0], key_rows[0], out_grad[0])
    near = lax.axis_size("zr")
    across = shift(tokens, "zq", 1)
    packed = attend(plan_of, queries[0], key_rows[0], value_rows[0], out_grad[0])
    pair = jnp.concatenate([tokens, across], axis=1)
    blocks = [pair]
    for k in range(1, near):
        blocks += [shift(pair, "zr", k)]
    received = lax.all_to_all(packed, ("zhi", "x"), split_axis=0, concat_axis=0, tiled=True)
    features, width = inputs.shape[2], sum(b.shape[1] for b in blocks)
    ny, nc, nz, nx = (lax.axis_size(a) for a in ("y", "core", "zhi", "x"))
    core = lax.axis_index("core").astype(jnp.int32).reshape(1)
    away, kept = terms(core, inputs[0], blocks, nc)
    came = shift(away, "core", 1)
    total = kept + came.astype(jnp.float32)
    total = total.reshape(ny, nz, nx, features // (ny * nc * nz * nx), width)
    total = fold(total, "y", 0)
    total = fold(total, "x", 1)
    total = fold_far(total, "zhi")
    total = total.reshape(-1, 2 * near, HD)
    zq, zr = lax.axis_index("zq"), lax.axis_index("zr")
    block = jnp.arange(2 * near)
    source = 2 * jnp.bitwise_and(zr - block, near - 1) + (block // near != zq)
    total = jnp.take(total, source, axis=1).reshape(-1, width)
    query_grad, key_grad, value_grad = finish(received, packed.shape[0] // doc_plan.shape[1])
    return (query_grad[None], key_grad[None], value_grad[None], total)


def solution(mesh):
    fine = Mesh(mesh.devices.reshape(4, 2, 4, 4, 2, 4), ("y", "core", "zhi", "x", "zq", "zr"))
    tokens = P(("y", "core", "zhi", "x"), None, ("zq", "zr"))
    groups = P(("y", "core"), None)

    return jax.shard_map(
        shards,
        mesh=fine,
        in_specs=(tokens, tokens, tokens, tokens, tokens, groups, groups),
        out_specs=(tokens, tokens, tokens, P(("zq", "zr", "y", "core", "zhi", "x"), None)),
        check_vma=False,
    )
```

```python
import functools

import jax
import jax.numpy as jnp
from jax import lax
from jax.experimental import pallas as pl
from jax.experimental.pallas import tpu as pltpu
from jax.sharding import Mesh, PartitionSpec as P


HD = 128
GROUP = 4
DOCS = 4
NEG = -1e30
LOW = jnp.bfloat16


def dot(a, b):
    return jnp.dot(a, b, preferred_element_type=jnp.float32)


def nt_dot(a, b):
    return lax.dot_general(a, b, (((1,), (1,)), ((), ())), preferred_element_type=jnp.float32)


def tn_dot(a, b):
    return lax.dot_general(a, b, (((0,), (0,)), ((), ())), preferred_element_type=jnp.float32)


def block_of(ids, capacity):
    block = jnp.zeros_like(ids)
    for d in range(1, DOCS):
        block = block + (ids >= d * capacity).astype(jnp.int32)
    return block


def iotas(rows, cols):
    return (
        lax.broadcasted_iota(jnp.int32, (rows, cols), 0),
        lax.broadcasted_iota(jnp.int32, (rows, cols), 1),
    )


def causal_mask(capacity):
    tile = DOCS * capacity
    rows, cols = iotas(tile, tile)
    return (cols <= rows) & (block_of(rows, capacity) == block_of(cols, capacity))


def one_hot(condition):
    return jnp.where(condition, 1.0, 0.0).astype(LOW)


def lane_maps(capacity):
    tile = DOCS * capacity
    cols, lanes = iotas(tile, HD)
    within = cols - capacity * block_of(cols, capacity)
    half = HD // 2
    upright = [one_hot(lanes == within), one_hot(lanes == within + half)]
    turned = [one_hot(lanes == capacity - within), one_hot(lanes == capacity - within + half)]
    return upright, turned


def flip_map(capacity):
    tile = DOCS * capacity
    rows, cols = iotas(tile, tile)
    block = block_of(rows, capacity)
    within = rows - capacity * block
    return one_hot(cols == block * capacity + (capacity - 1) - within)


def place_rows(index_ref, lengths_ref, plan_ref, place_ref, capacity):
    own = index_ref[0]
    offsets = lax.broadcasted_iota(jnp.int32, (capacity, HD), 0)
    start = jnp.int32(0)
    for d in range(lengths_ref.shape[1]):
        length = lengths_ref[own, d]
        target = plan_ref[own, d]
        place_ref[pl.ds(pl.multiple_of(target * capacity, 8), capacity), :] = jnp.where(
            offsets < length, start + offsets, -1
        )
        start = start + length


def fetch(pairs, sems):
    copies = [
        pltpu.make_async_copy(source, target, sems.at[i])
        for i, (source, target) in enumerate(pairs)
    ]
    for copy in copies:
        copy.start()
    return copies


def picker(place_ref, here, seq_len):
    place = jnp.concatenate([place_ref[here, :]] * (seq_len // HD), axis=1)
    return one_hot(place == lax.broadcasted_iota(jnp.int32, place.shape, 1))


def by_head(rows):
    return jnp.concatenate([rows[:, h * HD : (h + 1) * HD] for h in range(GROUP)], axis=0)


def softmax_bias(capacity):
    return jnp.concatenate([jnp.where(causal_mask(capacity), 0.0, NEG)] * GROUP, axis=0)


def softmax(query, key, bias):
    scores = nt_dot(query, key) * HD ** (-0.5) + bias
    raised = jnp.exp(scores - jnp.max(scores, axis=1, keepdims=True))
    return raised / jnp.sum(raised, axis=1, keepdims=True)


def tokens_kernel(
    index_ref,
    lengths_ref,
    plan_ref,
    query_hbm,
    key_hbm,
    grad_hbm,
    tokens_ref,
    query_ref,
    key_ref,
    grad_ref,
    sums_ref,
    sems,
):
    copies = fetch(((query_hbm, query_ref), (key_hbm, key_ref), (grad_hbm, grad_ref)), sems)
    own = index_ref[0]
    starts = [jnp.int32(0)]
    for d in range(lengths_ref.shape[1] - 1):
        starts.append(starts[-1] + lengths_ref[own, d])
    sums_ref[...] = jnp.zeros_like(sums_ref)
    for copy in copies:
        copy.wait()
    for tile in range(query_ref.shape[0] // HD):
        here = slice(tile * HD, (tile + 1) * HD)
        left = max(tile - 1, 0) * HD
        window = slice(left, (tile + 1) * HD)
        rows, cols = iotas(HD, here.stop - left)
        rows, cols = rows + here.start, cols + left
        first = jnp.zeros_like(rows)
        for start in starts[1:]:
            first = jnp.where(rows >= start, start, first)
        bias = jnp.where((cols <= rows) & (cols >= first), 0.0, NEG)
        bias = jnp.concatenate([bias] * GROUP, axis=0)
        probs = softmax(by_head(query_ref[here, :]), key_ref[window, :], bias)
        sums_ref[window, :] += tn_dot(probs.astype(LOW), by_head(grad_ref[here, :]))
    tokens_ref[...] = sums_ref[...].astype(LOW)


def attend_kernel(
    index_ref,
    lengths_ref,
    plan_ref,
    query_hbm,
    key_hbm,
    value_hbm,
    grad_hbm,
    packed_ref,
    query_ref,
    key_ref,
    value_ref,
    grad_ref,
    place_ref,
    sems,
):
    copies = fetch(
        (
            (query_hbm, query_ref),
            (key_hbm, key_ref),
            (value_hbm, value_ref),
            (grad_hbm, grad_ref),
        ),
        sems,
    )
    seq_len = query_ref.shape[0]
    capacity = place_ref.shape[0] // lengths_ref.shape[1]
    tile = DOCS * capacity
    scale = HD ** (-0.5)
    place_rows(index_ref, lengths_ref, plan_ref, place_ref, capacity)
    bias = softmax_bias(capacity)
    upright, turned = lane_maps(capacity)
    flip = flip_map(capacity)
    for copy in copies:
        copy.wait()
    for part in range(place_ref.shape[0] // tile):
        here = slice(part * tile, (part + 1) * tile)
        pick = picker(place_ref, here, seq_len)
        query = by_head(dot(pick, query_ref[...]).astype(LOW))
        grad = by_head(dot(pick, grad_ref[...]).astype(LOW))
        key = dot(pick, key_ref[...]).astype(LOW)
        value = dot(pick, value_ref[...]).astype(LOW)
        probs = softmax(query, key, bias)
        probs_low = probs.astype(LOW)
        prob_grad = nt_dot(grad, value)
        row_delta = jnp.sum(probs_low.astype(jnp.float32) * prob_grad, axis=1, keepdims=True)
        dscore = (probs * (prob_grad - row_delta)).astype(LOW)
        heads = [dscore[h * tile : (h + 1) * tile, :] for h in range(GROUP)]
        below = dot(heads[0], upright[0]) + dot(heads[1], upright[1])
        above = (dot(heads[2], turned[0]) + dot(heads[3], turned[1])).astype(LOW)
        packed_ref[here, 0:HD] = key
        packed_ref[here, HD : 2 * HD] = (tn_dot(dscore, query) * scale).astype(LOW)
        packed_ref[here, 2 * HD : 3 * HD] = tn_dot(probs_low, grad).astype(LOW)
        packed_ref[here, 3 * HD : 4 * HD] = (below + dot(flip, above)).astype(LOW)


def local_call(kernel, plan_of, arrays, out_shape, scratch, flops):
    seq_len = arrays[0].shape[0]
    docs = plan_of[1].shape[1]
    packed = docs * (5 * seq_len // (4 * docs))
    smem = pl.BlockSpec(memory_space=pltpu.SMEM)
    moved = sum(2 * a.size for a in arrays)
    return pl.pallas_call(
        kernel,
        out_shape=out_shape(packed),
        in_specs=[smem] * 3 + [pl.BlockSpec(memory_space=pl.ANY)] * len(arrays),
        out_specs=pl.BlockSpec(memory_space=pltpu.VMEM),
        scratch_shapes=[pltpu.VMEM(a.shape, LOW) for a in arrays]
        + [scratch(packed), pltpu.SemaphoreType.DMA((len(arrays),))],
        compiler_params=pltpu.CompilerParams(vmem_limit_bytes=60 << 20),
        cost_estimate=pl.CostEstimate(flops=flops, bytes_accessed=moved, transcendentals=400000),
    )(*plan_of, *arrays)


def value_tokens(plan_of, query, key, grad):
    return local_call(
        tokens_kernel,
        plan_of,
        (query, key, grad),
        lambda packed: jax.ShapeDtypeStruct(key.shape, LOW),
        lambda packed: pltpu.VMEM(key.shape, jnp.float32),
        10**9,
    )


def attend(plan_of, query, key, value, grad):
    return local_call(
        attend_kernel,
        plan_of,
        (query, key, value, grad),
        lambda packed: jax.ShapeDtypeStruct((packed, 4 * HD), LOW),
        lambda packed: pltpu.VMEM((packed, HD), jnp.int32),
        2 * 10**9,
    )


def finish_kernel(capacity, packed_ref, query_out, key_out, value_out):
    scale = HD ** (-0.5)
    mask = causal_mask(capacity)
    upright, turned = lane_maps(capacity)
    key = packed_ref[:, 0:HD]
    below = packed_ref[:, 3 * HD : 4 * HD]
    above = dot(flip_map(capacity), below).astype(LOW)
    for h, (half, lanes) in enumerate(
        ((below, upright[0]), (below, upright[1]), (above, turned[0]), (above, turned[1]))
    ):
        dscore = jnp.where(mask, nt_dot(half, lanes), 0.0).astype(LOW)
        query_out[:, h * HD : (h + 1) * HD] = (dot(dscore, key) * scale).astype(LOW)
    key_out[...] = packed_ref[:, HD : 2 * HD]
    value_out[...] = packed_ref[:, 2 * HD : 3 * HD]


def finish(received, capacity):
    rows = received.shape[0]
    tile = DOCS * capacity

    def spec(width):
        return pl.BlockSpec((tile, width), lambda i: (i, 0))

    return pl.pallas_call(
        functools.partial(finish_kernel, capacity),
        grid=(rows // tile,),
        out_shape=(
            jax.ShapeDtypeStruct((rows, GROUP * HD), LOW),
            jax.ShapeDtypeStruct((rows, HD), LOW),
            jax.ShapeDtypeStruct((rows, HD), LOW),
        ),
        in_specs=[spec(4 * HD)],
        out_specs=(spec(GROUP * HD), spec(HD), spec(HD)),
        compiler_params=pltpu.CompilerParams(vmem_limit_bytes=16 << 20),
        name="finish",
    )(received)


def term_kernel(core_ref, inputs_ref, *refs):
    *block_refs, away_ref, kept_ref = refs
    values = jnp.concatenate([ref[...] for ref in block_refs], axis=1)
    cores = inputs_ref.shape[1] // away_ref.shape[0]
    for out_ref, which in ((away_ref, cores - 1 - core_ref[0]), (kept_ref, core_ref[0])):
        for y in range(out_ref.shape[0] // HD):
            part = inputs_ref[:, pl.ds(pl.multiple_of((y * cores + which) * HD, HD), HD)]
            out_ref[y * HD : (y + 1) * HD, :] = tn_dot(part, values).astype(out_ref.dtype)


def terms(core, inputs, blocks, cores):
    rows, width = inputs.shape[1] // cores, sum(b.shape[1] for b in blocks)
    return pl.pallas_call(
        term_kernel,
        out_shape=(
            jax.ShapeDtypeStruct((rows, width), LOW),
            jax.ShapeDtypeStruct((rows, width), jnp.float32),
        ),
        in_specs=[pl.BlockSpec(memory_space=pltpu.SMEM)]
        + [pl.BlockSpec(memory_space=pltpu.VMEM)] * (1 + len(blocks)),
        out_specs=(pl.BlockSpec(memory_space=pltpu.VMEM),) * 2,
        compiler_params=pltpu.CompilerParams(vmem_limit_bytes=24 << 20),
        name="terms",
    )(core, inputs, *blocks)


def shift(value, axis, step):
    n = lax.axis_size(axis)
    return lax.ppermute(value, axis, [(i, (i + step) % n) for i in range(n)])


def pieces_kernel(choose, me_ref, own_ref, *refs):
    *others, total_ref = refs
    total = own_ref[...]
    picks = choose(me_ref[0])
    for came in others[: len(others) - len(picks)]:
        total = total + came[...].astype(jnp.float32)
    total_ref[...] = total
    for out_ref, blocks in zip(others[len(others) - len(picks) :], picks):
        size = out_ref.shape[0] // len(blocks)
        parts = [total_ref[pl.ds(pl.multiple_of(b * size, 8), size), :] for b in blocks]
        out_ref[...] = jnp.concatenate(parts, axis=0).astype(out_ref.dtype)


def pieces(axis, own, came, choose, shares):
    me = lax.axis_index(axis).astype(jnp.int32).reshape(1)
    rows, width = own.shape
    vmem = pl.BlockSpec(memory_space=pltpu.VMEM)
    return pl.pallas_call(
        functools.partial(pieces_kernel, choose),
        out_shape=tuple(
            jax.ShapeDtypeStruct((rows * of // total, width), dtype) for of, total, dtype in shares
        ),
        in_specs=[pl.BlockSpec(memory_space=pltpu.SMEM)] + [vmem] * (1 + len(came)),
        out_specs=(vmem,) * len(shares),
        scratch_shapes=[pltpu.VMEM((rows, width), jnp.float32)],
        compiler_params=pltpu.CompilerParams(vmem_limit_bytes=24 << 20),
        name="pieces",
    )(me, own, *came)


def exchange(axis, own, came, outer):
    n = lax.axis_size(axis)

    def choose(me):
        return [[z * n + lax.rem(me + step, n) for z in range(outer)] for step in range(n)]

    shares = [(1, n, jnp.float32)] + [(1, n, LOW)] * (n - 1)
    own, *parts = pieces(axis, own, came, choose, shares)
    got = []
    for step in range(1, n):
        got.append(shift(parts[step - 1], axis, step))
    return own, got


def exchange_far(axis, own, came):
    def choose(me):
        first = jnp.bitwise_xor(me, 1)
        return [[first, 3 - first], [me], [3 - me]]

    shares = [(2, 4, LOW), (1, 4, jnp.float32), (1, 4, jnp.float32)]
    away, mine, other = pieces(axis, own, came, choose, shares)
    got = lax.ppermute(away, axis, [(i, i ^ 1) for i in range(4)]).astype(jnp.float32)
    size = mine.shape[0]
    back = (other + got[size:]).astype(LOW)
    back = lax.ppermute(back, axis, [(i, 3 - i) for i in range(4)])
    return mine + got[:size] + back.astype(jnp.float32)


def shards(queries, key_rows, value_rows, out_grad, inputs, doc_lengths, doc_plan):
    own = lax.axis_index(("zhi", "x")).astype(jnp.int32).reshape(1)
    plan_of = (own, doc_lengths, doc_plan)
    tokens = value_tokens(plan_of, queries[0], key_rows[0], out_grad[0])
    near = lax.axis_size("zr")
    across = shift(tokens, "zq", 1)
    packed = attend(plan_of, queries[0], key_rows[0], value_rows[0], out_grad[0])
    pair = jnp.concatenate([tokens, across], axis=1)
    blocks = [pair]
    for k in range(1, near):
        blocks += [shift(pair, "zr", k)]
    received = lax.all_to_all(packed, ("zhi", "x"), split_axis=0, concat_axis=0, tiled=True)
    core = lax.axis_index("core").astype(jnp.int32).reshape(1)
    away, kept = terms(core, inputs[0], blocks, lax.axis_size("core"))
    came = shift(away, "core", 1)
    own_sum, got = exchange("y", kept, [came], 1)
    own_sum, got = exchange("x", own_sum, got, lax.axis_size("zhi"))
    total = exchange_far("zhi", own_sum, got)
    total = total.reshape(-1, 2 * near, HD)
    zq, zr = lax.axis_index("zq"), lax.axis_index("zr")
    block = jnp.arange(2 * near)
    source = 2 * jnp.bitwise_and(zr - block, near - 1) + (block // near != zq)
    total = jnp.take(total, source, axis=1).reshape(total.shape[0], -1)
    query_grad, key_grad, value_grad = finish(received, packed.shape[0] // doc_plan.shape[1])
    return (query_grad[None], key_grad[None], value_grad[None], total)


def solution(mesh):
    fine = Mesh(mesh.devices.reshape(4, 2, 4, 4, 2, 4), ("y", "core", "zhi", "x", "zq", "zr"))
    tokens = P(("y", "core", "zhi", "x"), None, ("zq", "zr"))
    groups = P(("y", "core"), None)

    return jax.shard_map(
        shards,
        mesh=fine,
        in_specs=(tokens, tokens, tokens, tokens, tokens, groups, groups),
        out_specs=(tokens, tokens, tokens, P(("zq", "zr", "y", "core", "zhi", "x"), None)),
        check_vma=False,
    )
```

```python
import functools

import jax
import jax.numpy as jnp
from jax import lax
from jax.experimental import pallas as pl
from jax.experimental.pallas import tpu as pltpu
from jax.sharding import Mesh, PartitionSpec as P


HD = 128
GROUP = 4
DOCS = 4
NEG = -1e30
LOW = jnp.bfloat16


def dot(a, b):
    return jnp.dot(a, b, preferred_element_type=jnp.float32)


def nt_dot(a, b):
    return lax.dot_general(a, b, (((1,), (1,)), ((), ())), preferred_element_type=jnp.float32)


def tn_dot(a, b):
    return lax.dot_general(a, b, (((0,), (0,)), ((), ())), preferred_element_type=jnp.float32)


def block_of(ids, capacity):
    block = jnp.zeros_like(ids)
    for d in range(1, DOCS):
        block = block + (ids >= d * capacity).astype(jnp.int32)
    return block


def iotas(rows, cols):
    return (
        lax.broadcasted_iota(jnp.int32, (rows, cols), 0),
        lax.broadcasted_iota(jnp.int32, (rows, cols), 1),
    )


def causal_mask(capacity):
    tile = DOCS * capacity
    rows, cols = iotas(tile, tile)
    return (cols <= rows) & (block_of(rows, capacity) == block_of(cols, capacity))


def one_hot(condition):
    return jnp.where(condition, 1.0, 0.0).astype(LOW)


def lane_maps(capacity):
    tile = DOCS * capacity
    cols, lanes = iotas(tile, HD)
    within = cols - capacity * block_of(cols, capacity)
    half = HD // 2
    upright = [one_hot(lanes == within), one_hot(lanes == within + half)]
    turned = [one_hot(lanes == capacity - within), one_hot(lanes == capacity - within + half)]
    return upright, turned


def flip_map(capacity):
    tile = DOCS * capacity
    rows, cols = iotas(tile, tile)
    block = block_of(rows, capacity)
    within = rows - capacity * block
    return one_hot(cols == block * capacity + (capacity - 1) - within)


def place_rows(index_ref, lengths_ref, plan_ref, place_ref, capacity):
    own = index_ref[0]
    offsets = lax.broadcasted_iota(jnp.int32, (capacity, HD), 0)
    start = jnp.int32(0)
    for d in range(lengths_ref.shape[1]):
        length = lengths_ref[own, d]
        target = plan_ref[own, d]
        place_ref[pl.ds(pl.multiple_of(target * capacity, 8), capacity), :] = jnp.where(
            offsets < length, start + offsets, -1
        )
        start = start + length


def fetch(pairs, sems):
    copies = [
        pltpu.make_async_copy(source, target, sems.at[i])
        for i, (source, target) in enumerate(pairs)
    ]
    for copy in copies:
        copy.start()
    return copies


def picker(place_ref, here, seq_len):
    place = jnp.concatenate([place_ref[here, :]] * (seq_len // HD), axis=1)
    return one_hot(place == lax.broadcasted_iota(jnp.int32, place.shape, 1))


def by_head(rows):
    return jnp.concatenate([rows[:, h * HD : (h + 1) * HD] for h in range(GROUP)], axis=0)


def softmax_bias(capacity):
    return jnp.concatenate([jnp.where(causal_mask(capacity), 0.0, NEG)] * GROUP, axis=0)


def softmax(query, key, bias):
    scores = nt_dot(query, key) * HD ** (-0.5) + bias
    raised = jnp.exp(scores - jnp.max(scores, axis=1, keepdims=True))
    return raised / jnp.sum(raised, axis=1, keepdims=True)


def tokens_kernel(
    index_ref,
    lengths_ref,
    plan_ref,
    query_hbm,
    key_hbm,
    grad_hbm,
    tokens_ref,
    query_ref,
    key_ref,
    grad_ref,
    sums_ref,
    sems,
):
    copies = fetch(((query_hbm, query_ref), (key_hbm, key_ref), (grad_hbm, grad_ref)), sems)
    own = index_ref[0]
    starts = [jnp.int32(0)]
    for d in range(lengths_ref.shape[1] - 1):
        starts.append(starts[-1] + lengths_ref[own, d])
    sums_ref[...] = jnp.zeros_like(sums_ref)
    for copy in copies:
        copy.wait()
    for tile in range(query_ref.shape[0] // HD):
        here = slice(tile * HD, (tile + 1) * HD)
        left = max(tile - 1, 0) * HD
        window = slice(left, (tile + 1) * HD)
        rows, cols = iotas(HD, here.stop - left)
        rows, cols = rows + here.start, cols + left
        first = jnp.zeros((HD, HD), jnp.int32)
        for start in starts[1:]:
            first = jnp.where(rows[:, :HD] >= start, start, first)
        first = jnp.concatenate([first] * (rows.shape[1] // HD), axis=1)
        bias = jnp.where((cols <= rows) & (cols >= first), 0.0, NEG)
        bias = jnp.concatenate([bias] * GROUP, axis=0)
        probs = softmax(by_head(query_ref[here, :]), key_ref[window, :], bias)
        sums_ref[window, :] += tn_dot(probs.astype(LOW), by_head(grad_ref[here, :]))
    tokens_ref[...] = sums_ref[...].astype(LOW)


def attend_kernel(
    index_ref,
    lengths_ref,
    plan_ref,
    query_hbm,
    key_hbm,
    value_hbm,
    grad_hbm,
    packed_ref,
    query_ref,
    key_ref,
    value_ref,
    grad_ref,
    place_ref,
    sems,
):
    copies = fetch(
        (
            (query_hbm, query_ref),
            (key_hbm, key_ref),
            (value_hbm, value_ref),
            (grad_hbm, grad_ref),
        ),
        sems,
    )
    seq_len = query_ref.shape[0]
    capacity = place_ref.shape[0] // lengths_ref.shape[1]
    tile = DOCS * capacity
    scale = HD ** (-0.5)
    place_rows(index_ref, lengths_ref, plan_ref, place_ref, capacity)
    bias = softmax_bias(capacity)
    upright, turned = lane_maps(capacity)
    flip = flip_map(capacity)
    for copy in copies:
        copy.wait()
    for part in range(place_ref.shape[0] // tile):
        here = slice(part * tile, (part + 1) * tile)
        pick = picker(place_ref, here, seq_len)
        query = by_head(dot(pick, query_ref[...]).astype(LOW))
        grad = by_head(dot(pick, grad_ref[...]).astype(LOW))
        key = dot(pick, key_ref[...]).astype(LOW)
        value = dot(pick, value_ref[...]).astype(LOW)
        probs = softmax(query, key, bias)
        probs_low = probs.astype(LOW)
        prob_grad = nt_dot(grad, value)
        row_delta = jnp.sum(probs_low.astype(jnp.float32) * prob_grad, axis=1, keepdims=True)
        dscore = (probs * (prob_grad - row_delta)).astype(LOW)
        heads = [dscore[h * tile : (h + 1) * tile, :] for h in range(GROUP)]
        below = dot(heads[0], upright[0]) + dot(heads[1], upright[1])
        above = (dot(heads[2], turned[0]) + dot(heads[3], turned[1])).astype(LOW)
        packed_ref[here, 0:HD] = key
        packed_ref[here, HD : 2 * HD] = (tn_dot(dscore, query) * scale).astype(LOW)
        packed_ref[here, 2 * HD : 3 * HD] = tn_dot(probs_low, grad).astype(LOW)
        packed_ref[here, 3 * HD : 4 * HD] = (below + dot(flip, above)).astype(LOW)


def local_call(kernel, plan_of, arrays, out_shape, scratch, flops):
    seq_len = arrays[0].shape[0]
    docs = plan_of[1].shape[1]
    packed = docs * (5 * seq_len // (4 * docs))
    smem = pl.BlockSpec(memory_space=pltpu.SMEM)
    moved = sum(2 * a.size for a in arrays)
    return pl.pallas_call(
        kernel,
        out_shape=out_shape(packed),
        in_specs=[smem] * 3 + [pl.BlockSpec(memory_space=pl.ANY)] * len(arrays),
        out_specs=pl.BlockSpec(memory_space=pltpu.VMEM),
        scratch_shapes=[pltpu.VMEM(a.shape, LOW) for a in arrays]
        + [scratch(packed), pltpu.SemaphoreType.DMA((len(arrays),))],
        compiler_params=pltpu.CompilerParams(vmem_limit_bytes=60 << 20),
        cost_estimate=pl.CostEstimate(flops=flops, bytes_accessed=moved, transcendentals=400000),
    )(*plan_of, *arrays)


def value_tokens(plan_of, query, key, grad):
    return local_call(
        tokens_kernel,
        plan_of,
        (query, key, grad),
        lambda packed: jax.ShapeDtypeStruct(key.shape, LOW),
        lambda packed: pltpu.VMEM(key.shape, jnp.float32),
        10**9,
    )


def attend(plan_of, query, key, value, grad):
    return local_call(
        attend_kernel,
        plan_of,
        (query, key, value, grad),
        lambda packed: jax.ShapeDtypeStruct((packed, 4 * HD), LOW),
        lambda packed: pltpu.VMEM((packed, HD), jnp.int32),
        2 * 10**9,
    )


def finish_kernel(capacity, packed_ref, query_out, key_out, value_out):
    scale = HD ** (-0.5)
    mask = causal_mask(capacity)
    upright, turned = lane_maps(capacity)
    key = packed_ref[:, 0:HD]
    below = packed_ref[:, 3 * HD : 4 * HD]
    above = dot(flip_map(capacity), below).astype(LOW)
    for h, (half, lanes) in enumerate(
        ((below, upright[0]), (below, upright[1]), (above, turned[0]), (above, turned[1]))
    ):
        dscore = jnp.where(mask, nt_dot(half, lanes), 0.0).astype(LOW)
        query_out[:, h * HD : (h + 1) * HD] = (dot(dscore, key) * scale).astype(LOW)
    key_out[...] = packed_ref[:, HD : 2 * HD]
    value_out[...] = packed_ref[:, 2 * HD : 3 * HD]


def finish(received, capacity):
    rows = received.shape[0]
    tile = DOCS * capacity

    def spec(width):
        return pl.BlockSpec((tile, width), lambda i: (i, 0))

    return pl.pallas_call(
        functools.partial(finish_kernel, capacity),
        grid=(rows // tile,),
        out_shape=(
            jax.ShapeDtypeStruct((rows, GROUP * HD), LOW),
            jax.ShapeDtypeStruct((rows, HD), LOW),
            jax.ShapeDtypeStruct((rows, HD), LOW),
        ),
        in_specs=[spec(4 * HD)],
        out_specs=(spec(GROUP * HD), spec(HD), spec(HD)),
        compiler_params=pltpu.CompilerParams(vmem_limit_bytes=16 << 20),
        name="finish",
    )(received)


def term_kernel(core_ref, inputs_ref, *refs):
    *block_refs, away_ref, kept_ref = refs
    values = jnp.concatenate([ref[...] for ref in block_refs], axis=1)
    cores = inputs_ref.shape[1] // away_ref.shape[0]
    for out_ref, which in ((away_ref, cores - 1 - core_ref[0]), (kept_ref, core_ref[0])):
        for y in range(out_ref.shape[0] // HD):
            part = inputs_ref[:, pl.ds(pl.multiple_of((y * cores + which) * HD, HD), HD)]
            out_ref[y * HD : (y + 1) * HD, :] = tn_dot(part, values).astype(out_ref.dtype)


def terms(core, inputs, blocks, cores):
    rows, width = inputs.shape[1] // cores, sum(b.shape[1] for b in blocks)
    return pl.pallas_call(
        term_kernel,
        out_shape=(
            jax.ShapeDtypeStruct((rows, width), LOW),
            jax.ShapeDtypeStruct((rows, width), jnp.float32),
        ),
        in_specs=[pl.BlockSpec(memory_space=pltpu.SMEM)]
        + [pl.BlockSpec(memory_space=pltpu.VMEM)] * (1 + len(blocks)),
        out_specs=(pl.BlockSpec(memory_space=pltpu.VMEM),) * 2,
        compiler_params=pltpu.CompilerParams(vmem_limit_bytes=24 << 20),
        name="terms",
    )(core, inputs, *blocks)


def shift(value, axis, step):
    n = lax.axis_size(axis)
    return lax.ppermute(value, axis, [(i, (i + step) % n) for i in range(n)])


def pieces_kernel(choose, columns, me_ref, own_ref, *refs):
    *others, total_ref, turned_ref = refs
    total = own_ref[...]
    picks = choose(me_ref[0])
    for came in others[: len(others) - len(picks)]:
        total = total + came[...].astype(jnp.float32)
    total_ref[...] = total
    if columns:
        for b in range(total.shape[1] // HD):
            at = pl.multiple_of(me_ref[1 + b] * HD, HD)
            turned_ref[:, b * HD : (b + 1) * HD] = total_ref[:, pl.ds(at, HD)]
        total_ref = turned_ref
    for out_ref, blocks in zip(others[len(others) - len(picks) :], picks):
        size = out_ref.shape[0] // len(blocks)
        parts = [total_ref[pl.ds(pl.multiple_of(b * size, 8), size), :] for b in blocks]
        out_ref[...] = jnp.concatenate(parts, axis=0).astype(out_ref.dtype)


def pieces(axis, own, came, choose, shares, columns=None):
    me = lax.axis_index(axis).astype(jnp.int32).reshape(1)
    if columns is not None:
        me = jnp.concatenate([me, columns])
    rows, width = own.shape
    vmem = pl.BlockSpec(memory_space=pltpu.VMEM)
    return pl.pallas_call(
        functools.partial(pieces_kernel, choose, columns is not None),
        out_shape=tuple(
            jax.ShapeDtypeStruct((rows * of // total, width), dtype) for of, total, dtype in shares
        ),
        in_specs=[pl.BlockSpec(memory_space=pltpu.SMEM)] + [vmem] * (1 + len(came)),
        out_specs=(vmem,) * len(shares),
        scratch_shapes=[pltpu.VMEM((rows, width), jnp.float32)] * 2,
        compiler_params=pltpu.CompilerParams(vmem_limit_bytes=24 << 20),
        name="pieces",
    )(me, own, *came)


def exchange(axis, own, came, outer):
    n = lax.axis_size(axis)

    def choose(me):
        return [[z * n + lax.rem(me + step, n) for z in range(outer)] for step in range(n)]

    shares = [(1, n, jnp.float32)] + [(1, n, LOW)] * (n - 1)
    own, *parts = pieces(axis, own, came, choose, shares)
    got = []
    for step in range(1, n):
        got.append(shift(parts[step - 1], axis, step))
    return own, got


def exchange_far(axis, own, came, columns):
    def choose(me):
        first = jnp.bitwise_xor(me, 1)
        return [[first, 3 - first], [me], [3 - me]]

    shares = [(2, 4, LOW), (1, 4, jnp.float32), (1, 4, jnp.float32)]
    away, mine, other = pieces(axis, own, came, choose, shares, columns)
    got = lax.ppermute(away, axis, [(i, i ^ 1) for i in range(4)]).astype(jnp.float32)
    size = mine.shape[0]
    back = (other + got[size:]).astype(LOW)
    back = lax.ppermute(back, axis, [(i, 3 - i) for i in range(4)])
    return mine + got[:size] + back.astype(jnp.float32)


def shards(queries, key_rows, value_rows, out_grad, inputs, doc_lengths, doc_plan):
    own = lax.axis_index(("zhi", "x")).astype(jnp.int32).reshape(1)
    plan_of = (own, doc_lengths, doc_plan)
    tokens = value_tokens(plan_of, queries[0], key_rows[0], out_grad[0])
    near = lax.axis_size("zr")
    across = shift(tokens, "zq", 1)
    packed = attend(plan_of, queries[0], key_rows[0], value_rows[0], out_grad[0])
    pair = jnp.concatenate([tokens, across], axis=1)
    blocks = [pair]
    for k in range(1, near):
        blocks += [shift(pair, "zr", k)]
    received = lax.all_to_all(packed, ("zhi", "x"), split_axis=0, concat_axis=0, tiled=True)
    core = lax.axis_index("core").astype(jnp.int32).reshape(1)
    away, kept = terms(core, inputs[0], blocks, lax.axis_size("core"))
    came = shift(away, "core", 1)
    own_sum, got = exchange("y", kept, [came], 1)
    own_sum, got = exchange("x", own_sum, got, lax.axis_size("zhi"))
    zq, zr = lax.axis_index("zq"), lax.axis_index("zr")
    block = jnp.arange(2 * near, dtype=jnp.int32)
    source = 2 * jnp.bitwise_and(zr - block, near - 1) + (block // near != zq)
    total = exchange_far("zhi", own_sum, got, source.astype(jnp.int32))
    query_grad, key_grad, value_grad = finish(received, packed.shape[0] // doc_plan.shape[1])
    return (query_grad[None], key_grad[None], value_grad[None], total)


def solution(mesh):
    fine = Mesh(mesh.devices.reshape(4, 2, 4, 4, 2, 4), ("y", "core", "zhi", "x", "zq", "zr"))
    tokens = P(("y", "core", "zhi", "x"), None, ("zq", "zr"))
    groups = P(("y", "core"), None)

    return jax.shard_map(
        shards,
        mesh=fine,
        in_specs=(tokens, tokens, tokens, tokens, tokens, groups, groups),
        out_specs=(tokens, tokens, tokens, P(("zq", "zr", "y", "core", "zhi", "x"), None)),
        check_vma=False,
    )
```
